256 devices in a mesh: ctx: 128 (over y, z, x_lo, core), head: 2 (over x_hi).
Axes of the slice: x: 4 (x_hi: 2, x_lo: 2; x = x_hi * 2 + x_lo), y: 4, z: 8, core: 2. Of those that a mesh axis runs over, the one named last changes fastest.
Arguments:
- queries: bfloat16 [16384, 2048], P('ctx', 'head'), may hold values from -6 to 6
- key_states: bfloat16 [16384, 512], P(('ctx', 'head')), may hold values from -6 to 6
- value_states: bfloat16 [16384, 512], P(('ctx', 'head')), may hold values from -6 to 6
- attn_out: bfloat16 [16384, 2048], P('ctx', 'head'), may hold values from -1.5 to 1.5
- grad_out: bfloat16 [16384, 2048], P('ctx', 'head'), may hold values from -24 to 24
- log_sum_exp: float32 [16, 16384], P('head', 'ctx')
- token_order: int32 [16384], P('ctx'), may hold values from 0 to 16383, as said below
- position: int32 [16384], P('ctx'), may hold values from 0 to 4095, as said below
Outputs:
- grad_queries: bfloat16 [16384, 2048], P('ctx', 'head')
- grad_keys: bfloat16 [16384, 512], P(('ctx', 'head'))
- grad_values: bfloat16 [16384, 512], P(('ctx', 'head'))
The draws below stay inside these ranges and needn't reach their ends.
Inputs may be any that keep to these rules, and one draw needn't show every extreme that they name: `token_order`: a permutation of the sequence positions; the 128 rows of ctx index d hold consecutive positions in increasing order, all within quarter d mod 4 of the sequence (quarter k holds positions k * 4096 to (k + 1) * 4096 - 1). Documents are runs of consecutive sequence positions that never cross a multiple of 4096; token_order[r] - position[r] is the sequence position where row r's document starts; some document fills a whole quarter.
All inputs are finite; a program needn't handle non-finite values.
Results may differ from the reference program's by a relative error of at most 0.0055.
Values may be sent and summed in bfloat16 or wider, within the bound.
No kernel may reach another device: no remote copies, remote signals or barrier semaphores. Data moves between devices by JAX's collectives and lax.ppermute only.
A program may use at most 64 MiB of HBM per device.

```python
import math
import jax
import jax.numpy as jnp
from jax import lax

HEAD_DIM = 128
HEADS = 16
KV_HEADS = 4
TOK_DEV = 128
TOKENS = 16384


def layout_tables(base_key):
    block_count = TOKENS // TOK_DEV
    per_quarter = block_count // 4
    raw = jax.random.randint(jax.random.fold_in(base_key, 101), (4, per_quarter), 0, 1 << 20, dtype=jnp.int32)
    distinct = raw * per_quarter + jnp.arange(per_quarter, dtype=jnp.int32)[None, :]
    ranks = jnp.argsort(distinct, axis=1, stable=True).astype(jnp.int32)
    quarter_base = jnp.arange(4, dtype=jnp.int32)[None, :] * per_quarter
    chosen = (quarter_base + jnp.transpose(ranks)).reshape(block_count)
    within = jnp.arange(TOK_DEV, dtype=jnp.int32)
    order_table = (chosen[:, None] * TOK_DEV + within[None, :]).reshape(TOKENS)
    random_cuts = jax.random.randint(jax.random.fold_in(base_key, 102), (3,), 1, TOKENS, dtype=jnp.int32)
    quarter_cuts = jnp.array([1, 2, 3], dtype=jnp.int32) * (TOKENS // 4)
    cuts = jnp.concatenate([random_cuts, quarter_cuts])
    places = jnp.arange(TOKENS, dtype=jnp.int32)
    starts = jnp.max(jnp.where(cuts[None, :] <= places[:, None], cuts[None, :], 0), axis=1)
    offsets = places - starts
    return (order_table, offsets[order_table])


def draw_token_order(key, part):
    return layout_tables(key)[0]


def draw_position(key, part):
    return layout_tables(key)[1]


def draw_log_sum_exp(key, part):
    offsets = layout_tables(key)[1]
    centre = jnp.log(offsets.astype(jnp.float32) + 1.0) + 0.5
    noise_key = jax.random.fold_in(key, 103)
    noise = jax.random.uniform(noise_key, (HEADS, TOKENS), jnp.float32, -0.5, 0.5)
    return (centre[None, :] + noise).astype(jnp.float32)


def levels(rng, shape, cuts, least, largest):
    gain = 1.0
    for axis_at, parts in cuts:
        draws = jax.random.uniform(jax.random.fold_in(jax.random.fold_in(rng, 6), axis_at), (parts,), jnp.float32, least / len(cuts), largest / len(cuts))
        gain = gain * jnp.repeat(jnp.exp(draws), shape[axis_at] // parts).reshape((-1,) + (1,) * (len(shape) - 1 - axis_at))
    return gain


def normal_values(rng, extent, scale, bound, split=(), held_as=jnp.bfloat16):
    factor_of = levels(rng, extent, split, -0.22, 0.18) if split else 1.0
    values = jax.random.normal(rng, extent, jnp.float32) * scale * factor_of
    return jnp.minimum(jnp.maximum(values, -bound), bound).astype(held_as)


def setup_inputs(seed: int = 0) -> dict:
    keys = jax.random.split(jax.random.key(seed), 9)
    queries = normal_values(keys[0], (TOKENS, HEADS * HEAD_DIM), 1.0, 6.0, ((0, 128), (1, 2)))
    key_states = normal_values(keys[1], (TOKENS, KV_HEADS * HEAD_DIM), 1.0, 6.0, ((0, 256),))
    value_states = normal_values(keys[2], (TOKENS, KV_HEADS * HEAD_DIM), 1.0, 6.0, ((0, 256),))
    attn_out = normal_values(keys[3], (TOKENS, HEADS * HEAD_DIM), 0.25, 1.5, ((0, 128), (1, 2)))
    grad_out = normal_values(keys[4], (TOKENS, HEADS * HEAD_DIM), 4.0, 24.0, ((0, 128), (1, 2)))
    log_sum_exp = draw_log_sum_exp(jax.random.fold_in(keys[8], 71), 0)
    token_order = draw_token_order(jax.random.fold_in(keys[8], 71), 0)
    position = draw_position(jax.random.fold_in(keys[8], 71), 0)
    return dict(queries=queries, key_states=key_states, value_states=value_states, attn_out=attn_out, grad_out=grad_out, log_sum_exp=log_sum_exp, token_order=token_order, position=position)


def reference(queries, key_states, value_states, attn_out, grad_out, log_sum_exp, token_order, position):
    group_size = HEADS // KV_HEADS
    score_scale = HEAD_DIM ** -0.5
    tokens = queries.shape[0]
    query_four = queries.astype(jnp.float32).reshape(tokens, KV_HEADS, group_size, HEAD_DIM)
    grad_four = grad_out.astype(jnp.float32).reshape(tokens, KV_HEADS, group_size, HEAD_DIM)
    output_four = attn_out.astype(jnp.float32).reshape(tokens, KV_HEADS, group_size, HEAD_DIM)
    out_dot = jnp.sum(grad_four * output_four, axis=3)
    keys_three = key_states.astype(jnp.float32).reshape(tokens, KV_HEADS, HEAD_DIM)
    values_three = value_states.astype(jnp.float32).reshape(tokens, KV_HEADS, HEAD_DIM)
    lse_three = log_sum_exp.reshape(KV_HEADS, group_size, tokens)
    first_seen = token_order - position
    block_rows = math.gcd(tokens, 256)
    highest = lax.Precision.HIGHEST

    def block_step(sums, block_index):
        key_sum, value_sum = sums
        offset = (block_index * block_rows).astype(jnp.int32)
        query_block = lax.dynamic_slice_in_dim(query_four, offset, block_rows)
        grad_block = lax.dynamic_slice_in_dim(grad_four, offset, block_rows)
        dot_block = lax.dynamic_slice_in_dim(out_dot, offset, block_rows)
        lse_block = lax.dynamic_slice_in_dim(lse_three, offset, block_rows, axis=2)
        last_block = lax.dynamic_slice_in_dim(token_order, offset, block_rows)
        first_block = lax.dynamic_slice_in_dim(first_seen, offset, block_rows)
        visible = (token_order[None, :] <= last_block[:, None]) & (token_order[None, :] >= first_block[:, None])
        scores = jnp.einsum("tkgd,nkd->kgtn", query_block, keys_three, precision=highest) * score_scale
        weights = jnp.where(visible[None, None], jnp.exp(scores - lse_block[..., None]), 0.0)
        weights_round = lax.optimization_barrier(weights.astype(jnp.bfloat16)).astype(jnp.float32)
        prob_grad = jnp.einsum("tkgd,nkd->kgtn", grad_block, values_three, precision=highest)
        dot_moved = jnp.transpose(dot_block, (1, 2, 0))
        score_grad = weights * (prob_grad - dot_moved[..., None]) * score_scale
        score_grad = lax.optimization_barrier(score_grad.astype(jnp.bfloat16)).astype(jnp.float32)
        query_grad = jnp.einsum("kgtn,nkd->tkgd", score_grad, keys_three, precision=highest)
        key_sum = key_sum + jnp.einsum("kgtn,tkgd->nkd", score_grad, query_block, precision=highest)
        value_sum = value_sum + jnp.einsum("kgtn,tkgd->nkd", weights_round, grad_block, precision=highest)
        return (key_sum, value_sum), query_grad

    zeros_three = jnp.zeros((tokens, KV_HEADS, HEAD_DIM), jnp.float32)
    indices = jnp.arange(tokens // block_rows, dtype=jnp.int32)
    sums, query_blocks = lax.scan(block_step, (zeros_three, zeros_three), indices)
    grad_queries = query_blocks.reshape(tokens, HEADS * HEAD_DIM).astype(jnp.bfloat16)
    grad_keys = sums[0].reshape(tokens, KV_HEADS * HEAD_DIM).astype(jnp.bfloat16)
    grad_values = sums[1].reshape(tokens, KV_HEADS * HEAD_DIM).astype(jnp.bfloat16)
    return (grad_queries, grad_keys, grad_values)
```

```python
import functools
import math

import jax
import jax.numpy as jnp
from jax import lax
from jax.experimental import pallas as pl
from jax.experimental.pallas import tpu as pltpu
from jax.sharding import PartitionSpec as P

HEAD_DIM = 128
QUARTERS = 4
GRID_Y = 4
GRID_Z = 8
ROW_SHIFTS = (0, 1, -1, 2)
COL_SHIFTS = (0, 1, -1, 2, -2, 3, -3, 4)
AUX = 16
LOG2E = math.log2(math.e)
SCALE = HEAD_DIM ** (-0.5)

VMEM_SPEC = pl.BlockSpec(memory_space=pltpu.VMEM)
SMEM_SPEC = pl.BlockSpec(memory_space=pltpu.SMEM)
NT = (((1,), (1,)), ((), ()))
NN = (((1,), (0,)), ((), ()))


def dot(a, b, dims):
    return lax.dot_general(a, b, dims, preferred_element_type=jnp.float32)


def shifted(value, along_y, along_z):
    pairs = []
    for y in range(GRID_Y):
        for z in range(GRID_Z):
            source = ((y + along_y) % GRID_Y) * GRID_Z + (z + along_z) % GRID_Z
            for quarter in range(QUARTERS):
                pairs.append((source * QUARTERS + quarter, (y * GRID_Z + z) * QUARTERS + quarter))
    return lax.ppermute(value, "ctx", pairs)


def swap_head(value):
    return lax.ppermute(value, "head", [(0, 1), (1, 0)])


def split_three(x):
    high = x.astype(jnp.bfloat16)
    rest = x - high.astype(jnp.float32)
    middle = rest.astype(jnp.bfloat16)
    low = (rest - middle.astype(jnp.float32)).astype(jnp.bfloat16)
    return high, middle, low


def split_place(x):
    return (x >> 7).astype(jnp.float32).astype(jnp.bfloat16), (x & 127).astype(jnp.float32).astype(jnp.bfloat16)


def pack_rows_kernel(q_ref, o_ref, g_ref, lse_ref, order_ref, position_ref, out_ref):
    rows, width = q_ref.shape
    out_ref[0:rows, :] = q_ref[...]
    out_ref[rows : 2 * rows, :] = g_ref[...]
    base = 2 * rows
    out_ref[base : base + AUX, :] = jnp.zeros((AUX, width), jnp.bfloat16)
    order = order_ref[...]
    first = order - position_ref[...]
    places = split_place(first) + split_place(order)
    for at, part in enumerate(places):
        out_ref[base + 6 : base + 7, at * rows : (at + 1) * rows] = part
    product = q_ref.shape[1] // HEAD_DIM
    for h in range(product):
        span = slice(h * HEAD_DIM, (h + 1) * HEAD_DIM)
        both = g_ref[:, span].astype(jnp.float32) * o_ref[:, span].astype(jnp.float32)
        out_dot = jnp.sum(jnp.transpose(both), axis=0, keepdims=True)
        for at, part in enumerate(split_three(lse_ref[h : h + 1, :])):
            out_ref[base + at : base + at + 1, span] = part
        for at, part in enumerate(split_three(out_dot)):
            out_ref[base + 3 + at : base + 4 + at, span] = part


def pick_kernel(head_ref, k_ref, v_ref, keep_ref, send_ref):
    width = k_ref.shape[1] // 2
    head = head_ref[0]

    def fill(mine, other):
        keep_ref[:, :width] = k_ref[:, mine * width : (mine + 1) * width]
        keep_ref[:, width:] = v_ref[:, mine * width : (mine + 1) * width]
        send_ref[:, :width] = k_ref[:, other * width : (other + 1) * width]
        send_ref[:, width:] = v_ref[:, other * width : (other + 1) * width]

    pl.when(head == 0)(lambda: fill(0, 1))
    pl.when(head != 0)(lambda: fill(1, 0))


def pack_cols_kernel(head_ref, keep_ref, got_ref, order_ref, out_ref):
    half, width = keep_ref.shape
    head = head_ref[0]

    @pl.when(head == 0)
    def _():
        out_ref[0:half, :] = keep_ref[...]
        out_ref[half : 2 * half, :] = got_ref[...]

    @pl.when(head != 0)
    def _():
        out_ref[0:half, :] = got_ref[...]
        out_ref[half : 2 * half, :] = keep_ref[...]

    base = 2 * half
    out_ref[base : base + AUX, :] = jnp.zeros((AUX, width), jnp.bfloat16)
    for at, part in enumerate(split_place(order_ref[...])):
        out_ref[base : base + 1, at * 2 * half : (at + 1) * 2 * half] = part


def grads_kernel(n_rows, n_cols, *refs):
    row_refs = refs[:n_rows]
    col_refs = refs[n_rows : n_rows + n_cols]
    dq_refs = refs[n_rows + n_cols : 2 * n_rows + n_cols]
    dkv_refs = refs[2 * n_rows + n_cols : 2 * n_rows + 2 * n_cols]
    qs, gs, lse_s, dot_s, first_s, last_s, ks, vs, kts, dqt, dk, dv, scal = refs[2 * n_rows + 2 * n_cols :]
    rows = 128
    heads = row_refs[0].shape[1] // HEAD_DIM
    kv_heads = col_refs[0].shape[1] // HEAD_DIM // 2
    group = heads // kv_heads
    wide = group * rows

    eye_i = lax.broadcasted_iota(jnp.int32, (rows, rows), 0)
    eye_j = lax.broadcasted_iota(jnp.int32, (rows, rows), 1)
    eye = (eye_i == eye_j).astype(jnp.float32).astype(jnp.bfloat16)

    for r, ref in enumerate(row_refs):
        base = 2 * rows
        for h in range(heads):
            span = slice(h * HEAD_DIM, (h + 1) * HEAD_DIM)
            qs[r, span, :] = ref[0:rows, span]
            gs[r, span, :] = ref[rows : 2 * rows, span]
        aux = ref[base : base + AUX, :].astype(jnp.float32)
        lse = (aux[0:1] + aux[1:2]) + aux[2:3]
        out_dot = (aux[3:4] + aux[4:5]) + aux[5:6]
        lse_s[r] = lse * LOG2E
        dot_s[r] = out_dot
        first = aux[6:7, 0:rows] * 128.0 + aux[6:7, rows : 2 * rows]
        last = aux[6:7, 2 * rows : 3 * rows] * 128.0 + aux[6:7, 3 * rows : 4 * rows]
        first = first.astype(jnp.int32)
        last = last.astype(jnp.int32)
        for g in range(group):
            first_s[r, :, g * rows : (g + 1) * rows] = first
            last_s[r, :, g * rows : (g + 1) * rows] = last
        scal[0, r] = jnp.min(last)
        scal[1, r] = jnp.max(last)
        scal[2, r] = jnp.min(first)
        scal[3, r] = jnp.max(first)
    for c, ref in enumerate(col_refs):
        base = rows
        for j in range(kv_heads):
            k = ref[0:rows, j * HEAD_DIM : (j + 1) * HEAD_DIM]
            ks[c, j] = k
            vs[c, j] = ref[0:rows, (kv_heads + j) * HEAD_DIM : (kv_heads + j + 1) * HEAD_DIM]
            kts[c, j] = dot(eye, k, NT).astype(jnp.bfloat16)
        aux = ref[base : base + AUX, :].astype(jnp.float32)
        place = (aux[0:1, 0:rows] * 128.0 + aux[0:1, rows : 2 * rows]).astype(jnp.int32)
        scal[4, c] = jnp.min(place)
    dqt[...] = jnp.zeros_like(dqt)
    dk[...] = jnp.zeros_like(dk)
    dv[...] = jnp.zeros_like(dv)

    def tile(r, c, start, masked):
        if masked:
            place = start + lax.broadcasted_iota(jnp.int32, (rows, wide), 0)
            visible = (place <= last_s[r]) & (place >= first_s[r])
        for j in range(kv_heads):
            span = slice(j * wide, (j + 1) * wide)
            q = qs[r, span, :]
            g = gs[r, span, :]
            scores = dot(ks[c, j], q, NT)
            prob_grad = dot(vs[c, j], g, NT)
            probs = jnp.exp2(scores * (SCALE * LOG2E) - lse_s[r, :, span])
            if masked:
                probs = jnp.where(visible, probs, 0.0)
            score_grad = (probs * (prob_grad - dot_s[r, :, span]) * SCALE).astype(jnp.bfloat16)
            probs = probs.astype(jnp.bfloat16)
            dv[c, j] += dot(probs, g, NN)
            dk[c, j] += dot(score_grad, q, NN)
            dqt[r, j] += dot(kts[c, j], score_grad, NN)

    def step(at, carry):
        r = at // n_cols
        c = at % n_cols
        start = scal[4, c]
        end = start + rows - 1
        some = (start <= scal[1, r]) & (end >= scal[2, r])
        whole = (end <= scal[0, r]) & (start >= scal[3, r])
        pl.when(whole)(lambda: tile(r, c, start, False))
        pl.when(some & jnp.logical_not(whole))(lambda: tile(r, c, start, True))
        return carry

    lax.fori_loop(0, n_rows * n_cols, step, 0)

    for r, ref in enumerate(dq_refs):
        for j in range(kv_heads):
            for g in range(group):
                part = dqt[r, j, :, g * rows : (g + 1) * rows].astype(jnp.bfloat16)
                h = j * group + g
                ref[:, h * HEAD_DIM : (h + 1) * HEAD_DIM] = dot(eye, part, NT).astype(jnp.bfloat16)
    for c, ref in enumerate(dkv_refs):
        for j in range(kv_heads):
            ref[:, j * HEAD_DIM : (j + 1) * HEAD_DIM] = dk[c, j].astype(jnp.bfloat16)
            ref[:, (kv_heads + j) * HEAD_DIM : (kv_heads + j + 1) * HEAD_DIM] = dv[c, j].astype(jnp.bfloat16)


def shards(queries, key_states, value_states, attn_out, grad_out, log_sum_exp, token_order, position):
    rows, width = queries.shape
    half, all_width = key_states.shape
    kv_width = all_width // 2
    head = lax.axis_index("head").astype(jnp.int32)[None]
    order = token_order[None]
    shape = jax.ShapeDtypeStruct

    keep, send = pl.pallas_call(
        pick_kernel,
        out_shape=(shape((half, 2 * kv_width), jnp.bfloat16),) * 2,
        in_specs=[SMEM_SPEC, VMEM_SPEC, VMEM_SPEC],
        out_specs=(VMEM_SPEC,) * 2,
    )(head, key_states, value_states)
    got = swap_head(send)
    row_pack = pl.pallas_call(
        pack_rows_kernel,
        out_shape=shape((2 * rows + AUX, width), jnp.bfloat16),
        in_specs=[VMEM_SPEC] * 6,
        out_specs=VMEM_SPEC,
    )(queries, attn_out, grad_out, log_sum_exp, order, position[None])
    col_pack = pl.pallas_call(
        pack_cols_kernel,
        out_shape=shape((2 * half + AUX, 2 * kv_width), jnp.bfloat16),
        in_specs=[SMEM_SPEC, VMEM_SPEC, VMEM_SPEC, VMEM_SPEC],
        out_specs=VMEM_SPEC,
    )(head, keep, got, order)

    row_packs = [row_pack] + [shifted(row_pack, s, 0) for s in ROW_SHIFTS[1:]]
    ahead = [col_pack]
    behind = [col_pack]
    for _ in range(GRID_Z // 2 - 1):
        ahead.append(shifted(ahead[-1], 0, 1))
        behind.append(shifted(behind[-1], 0, -1))
    ahead.append(shifted(ahead[-1], 0, 1))
    col_packs = [ahead[s] if s >= 0 else behind[-s] for s in COL_SHIFTS]

    n_rows, n_cols = len(ROW_SHIFTS), len(COL_SHIFTS)
    kv_heads = kv_width // HEAD_DIM
    heads = width // HEAD_DIM
    wide = heads // kv_heads * rows
    outs = pl.pallas_call(
        functools.partial(grads_kernel, n_rows, n_cols),
        out_shape=(shape((rows, width), jnp.bfloat16),) * n_rows
        + (shape((rows, 2 * kv_width), jnp.bfloat16),) * n_cols,
        in_specs=[VMEM_SPEC] * (n_rows + n_cols),
        out_specs=(VMEM_SPEC,) * (n_rows + n_cols),
        scratch_shapes=[
            pltpu.VMEM((n_rows, heads * rows, HEAD_DIM), jnp.bfloat16),
            pltpu.VMEM((n_rows, heads * rows, HEAD_DIM), jnp.bfloat16),
            pltpu.VMEM((n_rows, 1, heads * rows), jnp.float32),
            pltpu.VMEM((n_rows, 1, heads * rows), jnp.float32),
            pltpu.VMEM((n_rows, 1, wide), jnp.int32),
            pltpu.VMEM((n_rows, 1, wide), jnp.int32),
            pltpu.VMEM((n_cols, kv_heads, rows, HEAD_DIM), jnp.bfloat16),
            pltpu.VMEM((n_cols, kv_heads, rows, HEAD_DIM), jnp.bfloat16),
            pltpu.VMEM((n_cols, kv_heads, HEAD_DIM, rows), jnp.bfloat16),
            pltpu.VMEM((n_rows, kv_heads, HEAD_DIM, wide), jnp.float32),
            pltpu.VMEM((n_cols, kv_heads, rows, HEAD_DIM), jnp.float32),
            pltpu.VMEM((n_cols, kv_heads, rows, HEAD_DIM), jnp.float32),
            pltpu.SMEM((5, n_cols), jnp.int32),
        ],
        compiler_params=pltpu.CompilerParams(vmem_limit_bytes=40 * 1024 * 1024),
    )(*row_packs, *col_packs)
    dq_parts, dkv_parts = outs[:n_rows], outs[n_rows:]

    dkv = dkv_parts[0].astype(jnp.float32)
    for s, part in list(zip(COL_SHIFTS, dkv_parts))[1:]:
        dkv = dkv + shifted(part, 0, -s).astype(jnp.float32)
    dq = dq_parts[0].astype(jnp.float32)
    for s, part in list(zip(ROW_SHIFTS, dq_parts))[1:]:
        dq = dq + shifted(part, -s, 0).astype(jnp.float32)
    grad_queries = dq.astype(jnp.bfloat16)

    dkv = dkv.astype(jnp.bfloat16)
    is_first = head[0] == 0
    send_back = jnp.where(is_first, dkv[half:], dkv[:half])
    mine = jnp.where(is_first, dkv[:half], dkv[half:])
    other = swap_head(send_back)
    low = jnp.where(is_first, mine, other)
    high = jnp.where(is_first, other, mine)
    grad_keys = jnp.concatenate([low[:, :kv_width], high[:, :kv_width]], axis=1)
    grad_values = jnp.concatenate([low[:, kv_width:], high[:, kv_width:]], axis=1)
    return grad_queries, grad_keys, grad_values


def solution(mesh):
    in_specs = (
        P("ctx", "head"),
        P(("ctx", "head"), None),
        P(("ctx", "head"), None),
        P("ctx", "head"),
        P("ctx", "head"),
        P("head", "ctx"),
        P("ctx"),
        P("ctx"),
    )
    out_specs = (P("ctx", "head"), P(("ctx", "head"), None), P(("ctx", "head"), None))
    return jax.shard_map(shards, mesh=mesh, in_specs=in_specs, out_specs=out_specs, check_vma=False)
```

```python
import functools
import math

import jax
import jax.numpy as jnp
from jax import lax
from jax.experimental import pallas as pl
from jax.experimental.pallas import tpu as pltpu
from jax.sharding import PartitionSpec as P


HEAD_DIM = 128
QUARTERS = 4
GRID_Y = 4
GRID_Z = 8
ROW_SHIFTS = (0, 1, -1, 2)
AUX = 16
LOG2E = math.log2(math.e)
SCALE = HEAD_DIM ** (-0.5)

VMEM_SPEC = pl.BlockSpec(memory_space=pltpu.VMEM)
SMEM_SPEC = pl.BlockSpec(memory_space=pltpu.SMEM)
NT = (((1,), (1,)), ((), ()))
NN = (((1,), (0,)), ((), ()))


def dot(a, b, dims):
    return lax.dot_general(a, b, dims, preferred_element_type=jnp.float32)


def shifted(value, along_y, along_z):
    pairs = []
    for y in range(GRID_Y):
        for z in range(GRID_Z):
            source = ((y + along_y) % GRID_Y) * GRID_Z + (z + along_z) % GRID_Z
            for quarter in range(QUARTERS):
                pairs.append((source * QUARTERS + quarter, (y * GRID_Z + z) * QUARTERS + quarter))
    return lax.ppermute(value, "ctx", pairs)


def swap_head(value):
    return lax.ppermute(value, "head", [(0, 1), (1, 0)])


def split_three(x):
    high = x.astype(jnp.bfloat16)
    rest = x - high.astype(jnp.float32)
    middle = rest.astype(jnp.bfloat16)
    low = (rest - middle.astype(jnp.float32)).astype(jnp.bfloat16)
    return high, middle, low


def split_place(x):
    return (x >> 7).astype(jnp.float32).astype(jnp.bfloat16), (x & 127).astype(jnp.float32).astype(jnp.bfloat16)


def pack_rows_kernel(q_ref, o_ref, g_ref, lse_ref, order_ref, position_ref, out_ref):
    rows, width = q_ref.shape
    out_ref[0:rows, :] = q_ref[...]
    out_ref[rows : 2 * rows, :] = g_ref[...]
    base = 2 * rows
    out_ref[base : base + AUX, :] = jnp.zeros((AUX, width), jnp.bfloat16)
    order = order_ref[...]
    first = order - position_ref[...]
    places = split_place(first) + split_place(order)
    for at, part in enumerate(places):
        out_ref[base + 6 : base + 7, at * rows : (at + 1) * rows] = part
    product = q_ref.shape[1] // HEAD_DIM
    for h in range(product):
        span = slice(h * HEAD_DIM, (h + 1) * HEAD_DIM)
        both = g_ref[:, span].astype(jnp.float32) * o_ref[:, span].astype(jnp.float32)
        out_dot = jnp.sum(jnp.transpose(both), axis=0, keepdims=True)
        for at, part in enumerate(split_three(lse_ref[h : h + 1, :])):
            out_ref[base + at : base + at + 1, span] = part
        for at, part in enumerate(split_three(out_dot)):
            out_ref[base + 3 + at : base + 4 + at, span] = part


def pick_kernel(head_ref, k_ref, v_ref, keep_ref, send_ref):
    width = k_ref.shape[1] // 2
    head = head_ref[0]

    def fill(mine, other):
        keep_ref[:, :width] = k_ref[:, mine * width : (mine + 1) * width]
        keep_ref[:, width:] = v_ref[:, mine * width : (mine + 1) * width]
        send_ref[:, :width] = k_ref[:, other * width : (other + 1) * width]
        send_ref[:, width:] = v_ref[:, other * width : (other + 1) * width]

    pl.when(head == 0)(lambda: fill(0, 1))
    pl.when(head != 0)(lambda: fill(1, 0))


def pack_cols_kernel(head_ref, keep_ref, got_ref, order_ref, out_ref):
    half, width = keep_ref.shape
    head = head_ref[0]

    @pl.when(head == 0)
    def _():
        out_ref[0:half, :] = keep_ref[...]
        out_ref[half : 2 * half, :] = got_ref[...]

    @pl.when(head != 0)
    def _():
        out_ref[0:half, :] = got_ref[...]
        out_ref[half : 2 * half, :] = keep_ref[...]

    base = 2 * half
    out_ref[base : base + AUX, :] = jnp.zeros((AUX, width), jnp.bfloat16)
    for at, part in enumerate(split_place(order_ref[...])):
        out_ref[base : base + 1, at * 2 * half : (at + 1) * 2 * half] = part


def grads_kernel(n_rows, col_places, done_rows, done_cols, given, final, *refs):
    n_cols = len(col_places)
    n_col_refs = 1 + max(at for at, _ in col_places)
    refs = list(refs)

    def take(count):
        taken, refs[:] = refs[:count], refs[count:]
        return taken

    row_refs = take(n_rows)
    col_refs = take(n_col_refs)
    sums_in = take(3) if given else None
    if final:
        dq_refs = take(n_rows)
        dkv_refs = take(n_cols)
    else:
        sums_out = take(3)
    qs, gs, lse_s, dot_s, first_s, last_s, ks, vs, kts = take(9)
    if final:
        dqt, dk, dv = take(3)
    else:
        dqt, dk, dv = sums_out
    starts, listed, counts = take(3)
    rows = 128
    heads = row_refs[0].shape[1] // HEAD_DIM
    kv_heads = col_refs[0].shape[1] // HEAD_DIM // 2
    group = heads // kv_heads
    wide = group * rows

    eye_i = lax.broadcasted_iota(jnp.int32, (rows, rows), 0)
    eye_j = lax.broadcasted_iota(jnp.int32, (rows, rows), 1)
    eye = (eye_i == eye_j).astype(jnp.float32).astype(jnp.bfloat16)

    col_starts = []
    for c, (at, base) in enumerate(col_places):
        ref = col_refs[at]
        for j in range(kv_heads):
            k = ref[base : base + rows, j * HEAD_DIM : (j + 1) * HEAD_DIM]
            ks[c, j] = k
            vs[c, j] = ref[base : base + rows, (kv_heads + j) * HEAD_DIM : (kv_heads + j + 1) * HEAD_DIM]
            kts[c, j] = dot(eye, k, NT).astype(jnp.bfloat16)
        aux = ref[base + rows : base + rows + AUX, :].astype(jnp.float32)
        place = (aux[0:1, 0:rows] * 128.0 + aux[0:1, rows : 2 * rows]).astype(jnp.int32)
        col_starts.append(jnp.min(place))
        starts[c] = col_starts[-1]
    for r, ref in enumerate(row_refs):
        base = 2 * rows
        for h in range(heads):
            span = slice(h * HEAD_DIM, (h + 1) * HEAD_DIM)
            qs[r, span, :] = ref[0:rows, span]
            gs[r, span, :] = ref[rows : 2 * rows, span]
        aux = ref[base : base + AUX, :].astype(jnp.float32)
        lse = (aux[0:1] + aux[1:2]) + aux[2:3]
        out_dot = (aux[3:4] + aux[4:5]) + aux[5:6]
        lse_s[r] = lse * LOG2E
        dot_s[r] = out_dot
        first = aux[6:7, 0:rows] * 128.0 + aux[6:7, rows : 2 * rows]
        last = aux[6:7, 2 * rows : 3 * rows] * 128.0 + aux[6:7, 3 * rows : 4 * rows]
        first = first.astype(jnp.int32)
        last = last.astype(jnp.int32)
        for g in range(group):
            first_s[r, :, g * rows : (g + 1) * rows] = first
            last_s[r, :, g * rows : (g + 1) * rows] = last
        most = jnp.max(last)
        least = jnp.min(first)
        count = jnp.int32(0)
        for c in range(n_cols):
            if r < done_rows and c < done_cols:
                continue
            listed[r, count] = c
            some = (col_starts[c] <= most) & (col_starts[c] + (rows - 1) >= least)
            count = count + some.astype(jnp.int32)
        counts[r] = count
    if given:
        for old, new in zip(sums_in, (dqt, dk, dv)):
            have = old.shape[0]
            new[0:have] = old[...]
            new[have:] = jnp.zeros((new.shape[0] - have,) + new.shape[1:], jnp.float32)
    else:
        dqt[...] = jnp.zeros_like(dqt)
        dk[...] = jnp.zeros_like(dk)
        dv[...] = jnp.zeros_like(dv)

    def pair(r, one, two, start_one, start_two):
        along = lax.broadcasted_iota(jnp.int32, (rows, wide), 0)
        last = last_s[r]
        first = first_s[r]
        visible = [
            (along + start <= last) & (along + start >= first) for start in (start_one, start_two)
        ]
        for j in range(kv_heads):
            span = slice(j * wide, (j + 1) * wide)
            q = qs[r, span, :]
            g = gs[r, span, :]
            keys = jnp.concatenate([ks[one, j], ks[two, j]], axis=0)
            values = jnp.concatenate([vs[one, j], vs[two, j]], axis=0)
            keys_turned = jnp.concatenate([kts[one, j], kts[two, j]], axis=1)
            scores = dot(keys, q, NT)
            prob_grad = dot(values, g, NT)
            lse = lse_s[r, :, span]
            out_dot = dot_s[r, :, span]
            probs_both = []
            grads_both = []
            for at in range(2):
                part = slice(at * rows, (at + 1) * rows)
                probs = jnp.exp2(scores[part] * (SCALE * LOG2E) - lse)
                probs = jnp.where(visible[at], probs, 0.0)
                grads_both.append((probs * (prob_grad[part] - out_dot) * SCALE).astype(jnp.bfloat16))
                probs_both.append(probs.astype(jnp.bfloat16))
            probs = jnp.concatenate(probs_both, axis=0)
            score_grad = jnp.concatenate(grads_both, axis=0)
            value_update = dot(probs, g, NN)
            key_update = dot(score_grad, q, NN)
            dv[one, j] += value_update[:rows]
            dv[two, j] += value_update[rows:]
            dk[one, j] += key_update[:rows]
            dk[two, j] += key_update[rows:]
            dqt[r, j] += dot(keys_turned, score_grad, NN)

    def row_block(r, carry):
        count = counts[r]

        def trip(at, inner):
            one = listed[r, 2 * at]
            both = 2 * at + 1 < count
            two = jnp.where(both, listed[r, 2 * at + 1], one)
            pair(r, one, two, starts[one], jnp.where(both, starts[two], 1 << 20))
            return inner

        return lax.fori_loop(0, (count + 1) // 2, trip, carry)

    lax.fori_loop(0, n_rows, row_block, 0)

    if not final:
        return
    for c, ref in enumerate(dkv_refs):
        for j in range(kv_heads):
            ref[:, j * HEAD_DIM : (j + 1) * HEAD_DIM] = dk[c, j].astype(jnp.bfloat16)
            ref[:, (kv_heads + j) * HEAD_DIM : (kv_heads + j + 1) * HEAD_DIM] = dv[c, j].astype(jnp.bfloat16)
    for r, ref in enumerate(dq_refs):
        for j in range(kv_heads):
            for g in range(group):
                part = dqt[r, j, :, g * rows : (g + 1) * rows].astype(jnp.bfloat16)
                h = j * group + g
                ref[:, h * HEAD_DIM : (h + 1) * HEAD_DIM] = dot(eye, part, NT).astype(jnp.bfloat16)


def call_grads(row_packs, col_packs, col_places, done, sums, final, rows, width, kv_width):
    n_rows, n_cols = len(row_packs), len(col_places)
    kv_heads = kv_width // HEAD_DIM
    heads = width // HEAD_DIM
    wide = heads // kv_heads * rows
    shape = jax.ShapeDtypeStruct
    sum_shapes = (
        (n_rows, kv_heads, HEAD_DIM, wide),
        (n_cols, kv_heads, rows, HEAD_DIM),
        (n_cols, kv_heads, rows, HEAD_DIM),
    )
    if final:
        out_shape = (shape((rows, width), jnp.bfloat16),) * n_rows
        out_shape += (shape((rows, 2 * kv_width), jnp.bfloat16),) * n_cols
    else:
        out_shape = tuple(shape(s, jnp.float32) for s in sum_shapes)
    operands = (*row_packs, *col_packs, *sums)
    scratch = [
        pltpu.VMEM((n_rows, heads * rows, HEAD_DIM), jnp.bfloat16),
        pltpu.VMEM((n_rows, heads * rows, HEAD_DIM), jnp.bfloat16),
        pltpu.VMEM((n_rows, 1, heads * rows), jnp.float32),
        pltpu.VMEM((n_rows, 1, heads * rows), jnp.float32),
        pltpu.VMEM((n_rows, 1, wide), jnp.int32),
        pltpu.VMEM((n_rows, 1, wide), jnp.int32),
        pltpu.VMEM((n_cols, kv_heads, rows, HEAD_DIM), jnp.bfloat16),
        pltpu.VMEM((n_cols, kv_heads, rows, HEAD_DIM), jnp.bfloat16),
        pltpu.VMEM((n_cols, kv_heads, HEAD_DIM, rows), jnp.bfloat16),
    ]
    if final:
        scratch += [pltpu.VMEM(s, jnp.float32) for s in sum_shapes]
    scratch += [
        pltpu.SMEM((n_cols,), jnp.int32),
        pltpu.SMEM((n_rows, n_cols + 1), jnp.int32),
        pltpu.SMEM((n_rows,), jnp.int32),
    ]
    body = functools.partial(grads_kernel, n_rows, col_places, *done, bool(sums), final)
    return pl.pallas_call(
        body,
        out_shape=out_shape,
        in_specs=[VMEM_SPEC] * len(operands),
        out_specs=(VMEM_SPEC,) * len(out_shape),
        scratch_shapes=scratch,
        compiler_params=pltpu.CompilerParams(vmem_limit_bytes=40 * 1024 * 1024),
    )(*operands)


def shards(queries, key_states, value_states, attn_out, grad_out, log_sum_exp, token_order, position):
    rows, width = queries.shape
    half, all_width = key_states.shape
    kv_width = all_width // 2
    head = lax.axis_index("head").astype(jnp.int32)[None]
    order = token_order[None]
    shape = jax.ShapeDtypeStruct

    keep, send = pl.pallas_call(
        pick_kernel,
        out_shape=(shape((half, 2 * kv_width), jnp.bfloat16),) * 2,
        in_specs=[SMEM_SPEC, VMEM_SPEC, VMEM_SPEC],
        out_specs=(VMEM_SPEC,) * 2,
    )(head, key_states, value_states)
    got = swap_head(send)
    row_pack = pl.pallas_call(
        pack_rows_kernel,
        out_shape=shape((2 * rows + AUX, width), jnp.bfloat16),
        in_specs=[VMEM_SPEC] * 6,
        out_specs=VMEM_SPEC,
    )(queries, attn_out, grad_out, log_sum_exp, order, position[None])
    col_pack = pl.pallas_call(
        pack_cols_kernel,
        out_shape=shape((2 * half + AUX, 2 * kv_width), jnp.bfloat16),
        in_specs=[SMEM_SPEC, VMEM_SPEC, VMEM_SPEC, VMEM_SPEC],
        out_specs=VMEM_SPEC,
    )(head, keep, got, order)

    row_packs = [row_pack]
    for s in (1, -1, 2):
        row_packs.append(shifted(row_pack, s, 0))
    ahead = shifted(col_pack, 0, 1)
    behind = shifted(col_pack, 0, -1)
    across = shifted(col_pack, 0, 4)
    ahead_pair = shifted(jnp.concatenate([col_pack, ahead], axis=0), 0, 2)
    behind_pair = shifted(jnp.concatenate([col_pack, behind], axis=0), 0, -2)
    size = 2 * half + AUX
    near_places = ((0, 0), (1, 0), (2, 0), (3, 0))
    far_places = ((4, 0), (4, size), (5, 0), (5, size))
    col_shifts = (0, 1, -1, 4, 2, 3, -2, -3)
    near = [col_pack, ahead, behind, across]

    sums = call_grads(row_packs[:3], near, near_places, (0, 0), (), False, rows, width, kv_width)
    outs = call_grads(
        row_packs,
        near + [ahead_pair, behind_pair],
        near_places + far_places,
        (3, 4),
        sums,
        True,
        rows,
        width,
        kv_width,
    )
    n_rows = len(ROW_SHIFTS)
    dq_parts, dkv_parts = outs[:n_rows], outs[n_rows:]

    dkv = dkv_parts[0].astype(jnp.float32)
    for s, part in list(zip(col_shifts, dkv_parts))[1:]:
        back = shifted(part, 0, -s)
        dkv = dkv + back.astype(jnp.float32)
    dq = dq_parts[0].astype(jnp.float32)
    for s, part in list(zip(ROW_SHIFTS, dq_parts))[1:]:
        back = shifted(part, -s, 0)
        dq = dq + back.astype(jnp.float32)
    grad_queries = dq.astype(jnp.bfloat16)

    dkv = dkv.astype(jnp.bfloat16)
    is_first = head[0] == 0
    send_back = jnp.where(is_first, dkv[half:], dkv[:half])
    mine = jnp.where(is_first, dkv[:half], dkv[half:])
    other = swap_head(send_back)
    low = jnp.where(is_first, mine, other)
    high = jnp.where(is_first, other, mine)
    grad_keys = jnp.concatenate([low[:, :kv_width], high[:, :kv_width]], axis=1)
    grad_values = jnp.concatenate([low[:, kv_width:], high[:, kv_width:]], axis=1)
    return grad_queries, grad_keys, grad_values


def solution(mesh):
    in_specs = (
        P("ctx", "head"),
        P(("ctx", "head"), None),
        P(("ctx", "head"), None),
        P("ctx", "head"),
        P("ctx", "head"),
        P("head", "ctx"),
        P("ctx"),
        P("ctx"),
    )
    out_specs = (P("ctx", "head"), P(("ctx", "head"), None), P(("ctx", "head"), None))
    return jax.shard_map(shards, mesh=mesh, in_specs=in_specs, out_specs=out_specs, check_vma=False)
```

```python
import functools
import math

import jax
import jax.numpy as jnp
from jax import lax
from jax.experimental import pallas as pl
from jax.experimental.pallas import tpu as pltpu
from jax.sharding import PartitionSpec as P


HEAD_DIM = 128
QUARTERS = 4
GRID_Y = 4
GRID_Z = 8
ROW_SHIFTS = (0, 1, -1, 2)
AUX = 8
LOG2E = math.log2(math.e)
SCALE = HEAD_DIM ** (-0.5)

VMEM_SPEC = pl.BlockSpec(memory_space=pltpu.VMEM)
SMEM_SPEC = pl.BlockSpec(memory_space=pltpu.SMEM)
NT = (((1,), (1,)), ((), ()))
NN = (((1,), (0,)), ((), ()))


def dot(a, b, dims):
    return lax.dot_general(a, b, dims, preferred_element_type=jnp.float32)


def shifted(value, along_y, along_z):
    pairs = []
    for y in range(GRID_Y):
        for z in range(GRID_Z):
            source = ((y + along_y) % GRID_Y) * GRID_Z + (z + along_z) % GRID_Z
            for quarter in range(QUARTERS):
                pairs.append((source * QUARTERS + quarter, (y * GRID_Z + z) * QUARTERS + quarter))
    return lax.ppermute(value, "ctx", pairs)


def swap_head(value):
    return lax.ppermute(value, "head", [(0, 1), (1, 0)])


def split_three(x):
    high = x.astype(jnp.bfloat16)
    rest = x - high.astype(jnp.float32)
    middle = rest.astype(jnp.bfloat16)
    low = (rest - middle.astype(jnp.float32)).astype(jnp.bfloat16)
    return high, middle, low


def split_place(x):
    return (x >> 7).astype(jnp.float32).astype(jnp.bfloat16), (x & 127).astype(jnp.float32).astype(jnp.bfloat16)


def pack_rows_kernel(q_ref, o_ref, g_ref, lse_ref, order_ref, position_ref, out_ref):
    rows, width = q_ref.shape
    out_ref[0:rows, :] = q_ref[...]
    out_ref[rows : 2 * rows, :] = g_ref[...]
    base = 2 * rows
    out_ref[base : base + AUX, :] = jnp.zeros((AUX, width), jnp.bfloat16)
    order = order_ref[...]
    first = order - position_ref[...]
    places = split_place(first) + split_place(order)
    for at, part in enumerate(places):
        out_ref[base + 6 : base + 7, at * rows : (at + 1) * rows] = part
    product = q_ref.shape[1] // HEAD_DIM
    for h in range(product):
        span = slice(h * HEAD_DIM, (h + 1) * HEAD_DIM)
        both = g_ref[:, span].astype(jnp.float32) * o_ref[:, span].astype(jnp.float32)
        out_dot = jnp.sum(jnp.transpose(both), axis=0, keepdims=True)
        for at, part in enumerate(split_three(lse_ref[h : h + 1, :])):
            out_ref[base + at : base + at + 1, span] = part
        for at, part in enumerate(split_three(out_dot)):
            out_ref[base + 3 + at : base + 4 + at, span] = part


def grads_kernel(row_places, col_places, dq_given, kv_given, dq_final, kv_final, *refs):
    n_rows = len(row_places)
    n_cols = len(col_places)
    refs = list(refs)

    def take(count):
        taken, refs[:] = refs[:count], refs[count:]
        return taken

    row_refs = take(1 + max(at for place in row_places for at, _ in place))
    col_refs = take(1 + max(at for at, _ in col_places))
    dq_in = take(dq_given)
    kv_in = take(2 * kv_given)
    dq_refs = take(n_rows if dq_final else 1)
    dkv_refs = take(n_cols if kv_final else 2)
    qs, gs, lse_s, dot_s, first_s, last_s, ks, vs, kts = take(9)
    dqt = take(1)[0] if dq_final else dq_refs[0]
    dk, dv = take(2) if kv_final else dkv_refs
    starts, listed, counts = take(3)
    rows = 128
    heads = row_refs[0].shape[1] // HEAD_DIM
    kv_heads = col_refs[0].shape[1] // HEAD_DIM // 2
    group = heads // kv_heads
    wide = group * rows

    eye_i = lax.broadcasted_iota(jnp.int32, (rows, rows), 0)
    eye_j = lax.broadcasted_iota(jnp.int32, (rows, rows), 1)
    eye = (eye_i == eye_j).astype(jnp.float32).astype(jnp.bfloat16)

    col_starts = []
    for c, (at, base) in enumerate(col_places):
        ref = col_refs[at]
        for j in range(kv_heads):
            k = ref[base : base + rows, j * HEAD_DIM : (j + 1) * HEAD_DIM]
            ks[c, j] = k
            vs[c, j] = ref[base : base + rows, (kv_heads + j) * HEAD_DIM : (kv_heads + j + 1) * HEAD_DIM]
            kts[c, j] = dot(eye, k, NT).astype(jnp.bfloat16)
        aux = ref[base + rows : base + rows + AUX, :].astype(jnp.float32)
        place = (aux[0:1, 0:rows] * 128.0 + aux[0:1, rows : 2 * rows]).astype(jnp.int32)
        col_starts.append(jnp.min(place))
        starts[c] = col_starts[-1]
    for r, ((q_at, q_base), (g_at, g_base), (at, base)) in enumerate(row_places):
        for h in range(heads):
            span = slice(h * HEAD_DIM, (h + 1) * HEAD_DIM)
            qs[r, span, :] = row_refs[q_at][q_base : q_base + rows, span]
            gs[r, span, :] = row_refs[g_at][g_base : g_base + rows, span]
        aux = row_refs[at][base : base + AUX, :].astype(jnp.float32)
        lse = (aux[0:1] + aux[1:2]) + aux[2:3]
        out_dot = (aux[3:4] + aux[4:5]) + aux[5:6]
        lse_s[r] = lse * LOG2E
        dot_s[r] = out_dot
        first = aux[6:7, 0:rows] * 128.0 + aux[6:7, rows : 2 * rows]
        last = aux[6:7, 2 * rows : 3 * rows] * 128.0 + aux[6:7, 3 * rows : 4 * rows]
        first = first.astype(jnp.int32)
        last = last.astype(jnp.int32)
        for g in range(group):
            first_s[r, :, g * rows : (g + 1) * rows] = first
            last_s[r, :, g * rows : (g + 1) * rows] = last
        most = jnp.max(last)
        least = jnp.min(first)
        count = jnp.int32(0)
        for c in range(n_cols):
            listed[r, count] = c
            some = (col_starts[c] <= most) & (col_starts[c] + (rows - 1) >= least)
            count = count + some.astype(jnp.int32)
        counts[r] = count
    filled = 0
    for old in dq_in:
        dqt[filled : filled + old.shape[0]] = old[...]
        filled += old.shape[0]
    if filled == 0:
        dqt[...] = jnp.zeros_like(dqt)
    if kv_given:
        dk[...] = kv_in[0][...]
        dv[...] = kv_in[1][...]
    else:
        dk[...] = jnp.zeros_like(dk)
        dv[...] = jnp.zeros_like(dv)

    def pair(r, one, two, start_one, start_two):
        along = lax.broadcasted_iota(jnp.int32, (rows, wide), 0)
        last = last_s[r]
        first = first_s[r]
        visible = [
            (along + start <= last) & (along + start >= first) for start in (start_one, start_two)
        ]
        for j in range(kv_heads):
            span = slice(j * wide, (j + 1) * wide)
            q = qs[r, span, :]
            g = gs[r, span, :]
            keys = jnp.concatenate([ks[one, j], ks[two, j]], axis=0)
            values = jnp.concatenate([vs[one, j], vs[two, j]], axis=0)
            keys_turned = jnp.concatenate([kts[one, j], kts[two, j]], axis=1)
            scores = dot(keys, q, NT)
            prob_grad = dot(values, g, NT)
            lse = lse_s[r, :, span]
            out_dot = dot_s[r, :, span]
            probs_both = []
            grads_both = []
            for at in range(2):
                part = slice(at * rows, (at + 1) * rows)
                probs = jnp.exp2(scores[part] * (SCALE * LOG2E) - lse)
                probs = jnp.where(visible[at], probs, 0.0)
                grads_both.append((probs * (prob_grad[part] - out_dot) * SCALE).astype(jnp.bfloat16))
                probs_both.append(probs.astype(jnp.bfloat16))
            probs = jnp.concatenate(probs_both, axis=0)
            score_grad = jnp.concatenate(grads_both, axis=0)
            value_update = dot(probs, g, NN)
            key_update = dot(score_grad, q, NN)
            dv[one, j] += value_update[:rows]
            dv[two, j] += value_update[rows:]
            dk[one, j] += key_update[:rows]
            dk[two, j] += key_update[rows:]
            dqt[r, j] += dot(keys_turned, score_grad, NN)

    def row_block(r, carry):
        count = counts[r]

        def trip(at, inner):
            one = listed[r, 2 * at]
            both = 2 * at + 1 < count
            two = jnp.where(both, listed[r, 2 * at + 1], one)
            pair(r, one, two, starts[one], jnp.where(both, starts[two], 1 << 20))
            return inner

        return lax.fori_loop(0, (count + 1) // 2, trip, carry)

    lax.fori_loop(0, n_rows, row_block, 0)

    for c, ref in enumerate(dkv_refs if kv_final else ()):
        for j in range(kv_heads):
            ref[:, j * HEAD_DIM : (j + 1) * HEAD_DIM] = dk[c, j].astype(jnp.bfloat16)
            ref[:, (kv_heads + j) * HEAD_DIM : (kv_heads + j + 1) * HEAD_DIM] = dv[c, j].astype(jnp.bfloat16)
    for r, ref in enumerate(dq_refs if dq_final else ()):
        for j in range(kv_heads):
            for g in range(group):
                part = dqt[r, j, :, g * rows : (g + 1) * rows].astype(jnp.bfloat16)
                h = j * group + g
                ref[:, h * HEAD_DIM : (h + 1) * HEAD_DIM] = dot(eye, part, NT).astype(jnp.bfloat16)


def call_grads(row_packs, row_places, col_packs, col_places, dq_in, kv_in, dq_final, kv_final):
    rows = 128
    n_rows, n_cols = len(row_places), len(col_places)
    width, all_kv = row_packs[0].shape[1], col_packs[0].shape[1]
    kv_heads = all_kv // HEAD_DIM // 2
    heads = width // HEAD_DIM
    wide = heads // kv_heads * rows
    shape = jax.ShapeDtypeStruct
    dq_shape = (n_rows, kv_heads, HEAD_DIM, wide)
    kv_shape = (n_cols, kv_heads, rows, HEAD_DIM)
    out_shape = (shape(dq_shape, jnp.float32),)
    if dq_final:
        out_shape = (shape((rows, width), jnp.bfloat16),) * n_rows
    if kv_final:
        out_shape += (shape((rows, all_kv), jnp.bfloat16),) * n_cols
    else:
        out_shape += (shape(kv_shape, jnp.float32),) * 2
    operands = (*row_packs, *col_packs, *dq_in, *kv_in)
    scratch = [
        pltpu.VMEM((n_rows, heads * rows, HEAD_DIM), jnp.bfloat16),
        pltpu.VMEM((n_rows, heads * rows, HEAD_DIM), jnp.bfloat16),
        pltpu.VMEM((n_rows, 1, heads * rows), jnp.float32),
        pltpu.VMEM((n_rows, 1, heads * rows), jnp.float32),
        pltpu.VMEM((n_rows, 1, wide), jnp.int32),
        pltpu.VMEM((n_rows, 1, wide), jnp.int32),
        pltpu.VMEM((n_cols, kv_heads, rows, HEAD_DIM), jnp.bfloat16),
        pltpu.VMEM((n_cols, kv_heads, rows, HEAD_DIM), jnp.bfloat16),
        pltpu.VMEM((n_cols, kv_heads, HEAD_DIM, rows), jnp.bfloat16),
    ]
    if dq_final:
        scratch += [pltpu.VMEM(dq_shape, jnp.float32)]
    if kv_final:
        scratch += [pltpu.VMEM(kv_shape, jnp.float32)] * 2
    scratch += [
        pltpu.SMEM((n_cols,), jnp.int32),
        pltpu.SMEM((n_rows, n_cols + 1), jnp.int32),
        pltpu.SMEM((n_rows,), jnp.int32),
    ]
    body = functools.partial(
        grads_kernel, row_places, col_places, len(dq_in), bool(kv_in), dq_final, kv_final
    )
    outs = pl.pallas_call(
        body,
        out_shape=out_shape,
        in_specs=[VMEM_SPEC] * len(operands),
        out_specs=(VMEM_SPEC,) * len(out_shape),
        scratch_shapes=scratch,
        compiler_params=pltpu.CompilerParams(vmem_limit_bytes=40 * 1024 * 1024),
    )(*operands)
    cut = n_rows if dq_final else 1
    return outs[:cut], outs[cut:]


def shards(queries, key_states, value_states, attn_out, grad_out, log_sum_exp, token_order, position):
    rows, width = queries.shape
    half, all_width = key_states.shape
    kv_width = all_width // 2
    head = lax.axis_index("head").astype(jnp.int32)[None]
    order = token_order[None]
    shape = jax.ShapeDtypeStruct

    is_first = head[0] == 0
    lower = jnp.concatenate([key_states[:, :kv_width], value_states[:, :kv_width]], axis=1)
    upper = jnp.concatenate([key_states[:, kv_width:], value_states[:, kv_width:]], axis=1)
    got = swap_head(jnp.where(is_first, upper, lower))
    row_pack = pl.pallas_call(
        pack_rows_kernel,
        out_shape=shape((2 * rows + AUX, width), jnp.bfloat16),
        in_specs=[VMEM_SPEC] * 6,
        out_specs=VMEM_SPEC,
    )(queries, attn_out, grad_out, log_sum_exp, order, position[None])
    keep = jnp.where(is_first, lower, upper)
    places = jnp.concatenate([*split_place(token_order), jnp.zeros((2 * kv_width - 2 * rows,), jnp.bfloat16)])
    col_pack = jnp.concatenate(
        [
            jnp.where(is_first, keep, got),
            jnp.where(is_first, got, keep),
            jnp.broadcast_to(places[None], (AUX, 2 * kv_width)),
        ],
        axis=0,
    )

    row_ahead = shifted(row_pack, 1, 0)
    row_behind = shifted(row_pack, -1, 0)
    row_two_q = shifted(row_ahead[:rows], 1, 0)
    row_two_g = shifted(row_behind[rows:], -1, 0)
    ahead = shifted(col_pack, 0, 1)
    behind = shifted(col_pack, 0, -1)
    across = shifted(col_pack, 0, 4)
    ahead_pair = shifted(jnp.concatenate([col_pack, ahead], axis=0), 0, 2)
    behind_pair = shifted(jnp.concatenate([col_pack, behind], axis=0), 0, -2)

    size = 2 * half + AUX
    first_rows = [row_pack, row_ahead, row_behind]
    first_places = tuple(((r, 0), (r, rows), (r, 2 * rows)) for r in range(3))
    two_rows = [row_two_q, row_two_g]
    near = [col_pack, ahead, behind, across]
    near_places = ((0, 0), (1, 0), (2, 0), (3, 0))
    near_shifts = (0, 1, -1, 4)
    far = [ahead_pair, behind_pair]
    far_places = ((0, 0), (0, size), (1, 0), (1, size))
    far_shifts = (2, 3, -2, -3)
    two_place = ((0, 0), (1, 0), (1, rows))
    last_place = ((3, 0), (4, 0), (4, rows))

    dq_first, kv_near = call_grads(first_rows, first_places, near, near_places, (), (), False, False)
    dq_two, near_parts = call_grads(two_rows, (two_place,), near, near_places, (), kv_near, False, True)
    dq_parts, far_parts = call_grads(
        first_rows + two_rows, first_places + (last_place,), far, far_places, (*dq_first, *dq_two), (), True, True
    )

    parts = dict(zip(near_shifts + far_shifts, (*near_parts, *far_parts)))
    dkv = parts.pop(0).astype(jnp.float32)
    for s, part in parts.items():
        back = shifted(part, 0, -s)
        dkv = dkv + back.astype(jnp.float32)
    dq = dq_parts[0].astype(jnp.float32)
    for s, part in list(zip(ROW_SHIFTS, dq_parts))[1:]:
        back = shifted(part, -s, 0)
        dq = dq + back.astype(jnp.float32)
    grad_queries = dq.astype(jnp.bfloat16)

    dkv = dkv.astype(jnp.bfloat16)
    send_back = jnp.where(is_first, dkv[half:], dkv[:half])
    mine = jnp.where(is_first, dkv[:half], dkv[half:])
    other = swap_head(send_back)
    low = jnp.where(is_first, mine, other)
    high = jnp.where(is_first, other, mine)
    grad_keys = jnp.concatenate([low[:, :kv_width], high[:, :kv_width]], axis=1)
    grad_values = jnp.concatenate([low[:, kv_width:], high[:, kv_width:]], axis=1)
    return grad_queries, grad_keys, grad_values


def solution(mesh):
    in_specs = (
        P("ctx", "head"),
        P(("ctx", "head"), None),
        P(("ctx", "head"), None),
        P("ctx", "head"),
        P("ctx", "head"),
        P("head", "ctx"),
        P("ctx"),
        P("ctx"),
    )
    out_specs = (P("ctx", "head"), P(("ctx", "head"), None), P(("ctx", "head"), None))
    return jax.shard_map(shards, mesh=mesh, in_specs=in_specs, out_specs=out_specs, check_vma=False)
```

```python
import functools
import math

import jax
import jax.numpy as jnp
from jax import lax
from jax.experimental import pallas as pl
from jax.experimental.pallas import tpu as pltpu
from jax.sharding import PartitionSpec as P


HEAD_DIM = 128
QUARTERS = 4
GRID_Y = 4
GRID_Z = 8
ROW_SHIFTS = (0, 1, -1, 2)
AUX = 8
LOG2E = math.log2(math.e)
SCALE = HEAD_DIM ** (-0.5)

VMEM_SPEC = pl.BlockSpec(memory_space=pltpu.VMEM)
SMEM_SPEC = pl.BlockSpec(memory_space=pltpu.SMEM)
NT = (((1,), (1,)), ((), ()))
NN = (((1,), (0,)), ((), ()))


def dot(a, b, dims):
    return lax.dot_general(a, b, dims, preferred_element_type=jnp.float32)


def shifted(value, along_y, along_z):
    pairs = []
    for y in range(GRID_Y):
        for z in range(GRID_Z):
            source = ((y + along_y) % GRID_Y) * GRID_Z + (z + along_z) % GRID_Z
            for quarter in range(QUARTERS):
                pairs.append((source * QUARTERS + quarter, (y * GRID_Z + z) * QUARTERS + quarter))
    return lax.ppermute(value, "ctx", pairs)


def swap_head(value):
    return lax.ppermute(value, "head", [(0, 1), (1, 0)])


def split_three(x):
    high = x.astype(jnp.bfloat16)
    rest = x - high.astype(jnp.float32)
    middle = rest.astype(jnp.bfloat16)
    low = (rest - middle.astype(jnp.float32)).astype(jnp.bfloat16)
    return high, middle, low


def split_place(x):
    return (x >> 7).astype(jnp.float32).astype(jnp.bfloat16), (x & 127).astype(jnp.float32).astype(jnp.bfloat16)


def pack_rows_kernel(q_ref, o_ref, g_ref, lse_ref, order_ref, position_ref, out_ref):
    rows, width = q_ref.shape
    out_ref[0:rows, :] = q_ref[...]
    out_ref[rows : 2 * rows, :] = g_ref[...]
    base = 2 * rows
    out_ref[base : base + AUX, :] = jnp.zeros((AUX, width), jnp.bfloat16)
    order = order_ref[...]
    first = order - position_ref[...]
    places = split_place(first) + split_place(order)
    for at, part in enumerate(places):
        out_ref[base + 6 : base + 7, at * rows : (at + 1) * rows] = part
    product = q_ref.shape[1] // HEAD_DIM
    for h in range(product):
        span = slice(h * HEAD_DIM, (h + 1) * HEAD_DIM)
        both = g_ref[:, span].astype(jnp.float32) * o_ref[:, span].astype(jnp.float32)
        out_dot = jnp.sum(jnp.transpose(both), axis=0, keepdims=True)
        for at, part in enumerate(split_three(lse_ref[h : h + 1, :])):
            out_ref[base + at : base + at + 1, span] = part
        for at, part in enumerate(split_three(out_dot)):
            out_ref[base + 3 + at : base + 4 + at, span] = part


def grads_kernel(row_places, col_places, dq_given, kv_given, dq_final, kv_final, *refs):
    n_rows = len(row_places)
    n_cols = len(col_places)
    refs = list(refs)

    def take(count):
        taken, refs[:] = refs[:count], refs[count:]
        return taken

    row_refs = take(1 + max(at for place in row_places for at, _ in place))
    col_refs = take(1 + max(at for at, _ in col_places))
    dq_in = take(dq_given)
    kv_in = take(2 * kv_given)
    dq_refs = take(n_rows if dq_final else 1)
    dkv_refs = take(n_cols if kv_final else 2)
    qs, gs, lse_s, dot_s, first_s, last_s, ks, vs, kts = take(9)
    dqt = take(1)[0] if dq_final else dq_refs[0]
    dk, dv = take(2) if kv_final else dkv_refs
    starts, listed, counts = take(3)
    rows = 128
    heads = row_refs[0].shape[1] // HEAD_DIM
    kv_heads = col_refs[0].shape[1] // HEAD_DIM // 2
    group = heads // kv_heads
    wide = group * rows

    eye_i = lax.broadcasted_iota(jnp.int32, (rows, rows), 0)
    eye_j = lax.broadcasted_iota(jnp.int32, (rows, rows), 1)
    eye = (eye_i == eye_j).astype(jnp.float32).astype(jnp.bfloat16)

    col_starts = []
    for c, (at, base) in enumerate(col_places):
        ref = col_refs[at]
        for j in range(kv_heads):
            k = ref[base : base + rows, j * HEAD_DIM : (j + 1) * HEAD_DIM]
            ks[c, j] = k
            vs[c, j] = ref[base : base + rows, (kv_heads + j) * HEAD_DIM : (kv_heads + j + 1) * HEAD_DIM]
            kts[c, j] = dot(eye, k, NT).astype(jnp.bfloat16)
        aux = ref[base + rows : base + rows + AUX, :].astype(jnp.float32)
        place = (aux[0:1, 0:rows] * 128.0 + aux[0:1, rows : 2 * rows]).astype(jnp.int32)
        col_starts.append(jnp.min(place))
        starts[c] = col_starts[-1]
    for r, ((q_at, q_base), (g_at, g_base), (at, base)) in enumerate(row_places):
        for h in range(heads):
            span = slice(h * HEAD_DIM, (h + 1) * HEAD_DIM)
            qs[r, span, :] = row_refs[q_at][q_base : q_base + rows, span]
            gs[r, span, :] = row_refs[g_at][g_base : g_base + rows, span]
        aux = row_refs[at][base : base + AUX, :].astype(jnp.float32)
        lse = (aux[0:1] + aux[1:2]) + aux[2:3]
        out_dot = (aux[3:4] + aux[4:5]) + aux[5:6]
        lse_s[r] = lse * LOG2E
        dot_s[r] = out_dot
        first = aux[6:7, 0:rows] * 128.0 + aux[6:7, rows : 2 * rows]
        last = aux[6:7, 2 * rows : 3 * rows] * 128.0 + aux[6:7, 3 * rows : 4 * rows]
        first = first.astype(jnp.int32)
        last = last.astype(jnp.int32)
        for g in range(group):
            first_s[r, :, g * rows : (g + 1) * rows] = first
            last_s[r, :, g * rows : (g + 1) * rows] = last
        most = jnp.max(last)
        least = jnp.min(first)
        count = jnp.int32(0)
        for c in range(n_cols):
            listed[r, count] = c
            some = (col_starts[c] <= most) & (col_starts[c] + (rows - 1) >= least)
            count = count + some.astype(jnp.int32)
        counts[r] = count
    filled = 0
    for old in dq_in:
        dqt[filled : filled + old.shape[0]] = old[...]
        filled += old.shape[0]
    if filled == 0:
        dqt[...] = jnp.zeros_like(dqt)
    if kv_given:
        dk[...] = kv_in[0][...]
        dv[...] = kv_in[1][...]
    else:
        dk[...] = jnp.zeros_like(dk)
        dv[...] = jnp.zeros_like(dv)

    def pair(r, one, two, start_one, start_two):
        along = lax.broadcasted_iota(jnp.int32, (rows, wide), 0)
        last = last_s[r]
        first = first_s[r]
        visible = [
            (along + start <= last) & (along + start >= first) for start in (start_one, start_two)
        ]
        for j in range(kv_heads):
            span = slice(j * wide, (j + 1) * wide)
            q = qs[r, span, :]
            g = gs[r, span, :]
            keys = jnp.concatenate([ks[one, j], ks[two, j]], axis=0)
            values = jnp.concatenate([vs[one, j], vs[two, j]], axis=0)
            keys_turned = jnp.concatenate([kts[one, j], kts[two, j]], axis=1)
            scores = dot(keys, q, NT)
            prob_grad = dot(values, g, NT)
            lse = lse_s[r, :, span]
            out_dot = dot_s[r, :, span]
            probs_both = []
            grads_both = []
            for at in range(2):
                part = slice(at * rows, (at + 1) * rows)
                probs = jnp.exp2(scores[part] * (SCALE * LOG2E) - lse)
                probs = jnp.where(visible[at], probs, 0.0)
                grads_both.append((probs * (prob_grad[part] - out_dot) * SCALE).astype(jnp.bfloat16))
                probs_both.append(probs.astype(jnp.bfloat16))
            probs = jnp.concatenate(probs_both, axis=0)
            score_grad = jnp.concatenate(grads_both, axis=0)
            value_update = dot(probs, g, NN)
            key_update = dot(score_grad, q, NN)
            dv[one, j] += value_update[:rows]
            dv[two, j] += value_update[rows:]
            dk[one, j] += key_update[:rows]
            dk[two, j] += key_update[rows:]
            dqt[r, j] += dot(keys_turned, score_grad, NN)

    def row_block(r, carry):
        count = counts[r]

        def trip(at, inner):
            one = listed[r, 2 * at]
            both = 2 * at + 1 < count
            two = jnp.where(both, listed[r, 2 * at + 1], one)
            pair(r, one, two, starts[one], jnp.where(both, starts[two], 1 << 20))
            return inner

        return lax.fori_loop(0, (count + 1) // 2, trip, carry)

    lax.fori_loop(0, n_rows, row_block, 0)

    for c, ref in enumerate(dkv_refs if kv_final else ()):
        for j in range(kv_heads):
            ref[:, j * HEAD_DIM : (j + 1) * HEAD_DIM] = dk[c, j].astype(jnp.bfloat16)
            ref[:, (kv_heads + j) * HEAD_DIM : (kv_heads + j + 1) * HEAD_DIM] = dv[c, j].astype(jnp.bfloat16)
    for r, ref in enumerate(dq_refs if dq_final else ()):
        for j in range(kv_heads):
            for g in range(group):
                part = dqt[r, j, :, g * rows : (g + 1) * rows].astype(jnp.bfloat16)
                h = j * group + g
                ref[:, h * HEAD_DIM : (h + 1) * HEAD_DIM] = dot(eye, part, NT).astype(jnp.bfloat16)


def call_grads(row_packs, row_places, col_packs, col_places, dq_in, kv_in, dq_final, kv_final):
    rows = 128
    n_rows, n_cols = len(row_places), len(col_places)
    width, all_kv = row_packs[0].shape[1], col_packs[0].shape[1]
    kv_heads = all_kv // HEAD_DIM // 2
    heads = width // HEAD_DIM
    wide = heads // kv_heads * rows
    shape = jax.ShapeDtypeStruct
    dq_shape = (n_rows, kv_heads, HEAD_DIM, wide)
    kv_shape = (n_cols, kv_heads, rows, HEAD_DIM)
    out_shape = (shape(dq_shape, jnp.float32),)
    if dq_final:
        out_shape = (shape((rows, width), jnp.bfloat16),) * n_rows
    if kv_final:
        out_shape += (shape((rows, all_kv), jnp.bfloat16),) * n_cols
    else:
        out_shape += (shape(kv_shape, jnp.float32),) * 2
    operands = (*row_packs, *col_packs, *dq_in, *kv_in)
    scratch = [
        pltpu.VMEM((n_rows, heads * rows, HEAD_DIM), jnp.bfloat16),
        pltpu.VMEM((n_rows, heads * rows, HEAD_DIM), jnp.bfloat16),
        pltpu.VMEM((n_rows, 1, heads * rows), jnp.float32),
        pltpu.VMEM((n_rows, 1, heads * rows), jnp.float32),
        pltpu.VMEM((n_rows, 1, wide), jnp.int32),
        pltpu.VMEM((n_rows, 1, wide), jnp.int32),
        pltpu.VMEM((n_cols, kv_heads, rows, HEAD_DIM), jnp.bfloat16),
        pltpu.VMEM((n_cols, kv_heads, rows, HEAD_DIM), jnp.bfloat16),
        pltpu.VMEM((n_cols, kv_heads, HEAD_DIM, rows), jnp.bfloat16),
    ]
    if dq_final:
        scratch += [pltpu.VMEM(dq_shape, jnp.float32)]
    if kv_final:
        scratch += [pltpu.VMEM(kv_shape, jnp.float32)] * 2
    scratch += [
        pltpu.SMEM((n_cols,), jnp.int32),
        pltpu.SMEM((n_rows, n_cols + 1), jnp.int32),
        pltpu.SMEM((n_rows,), jnp.int32),
    ]
    body = functools.partial(
        grads_kernel, row_places, col_places, len(dq_in), bool(kv_in), dq_final, kv_final
    )
    outs = pl.pallas_call(
        body,
        out_shape=out_shape,
        in_specs=[VMEM_SPEC] * len(operands),
        out_specs=(VMEM_SPEC,) * len(out_shape),
        scratch_shapes=scratch,
        compiler_params=pltpu.CompilerParams(vmem_limit_bytes=40 * 1024 * 1024),
    )(*operands)
    cut = n_rows if dq_final else 1
    return outs[:cut], outs[cut:]


def shards(queries, key_states, value_states, attn_out, grad_out, log_sum_exp, token_order, position):
    rows, width = queries.shape
    half, all_width = key_states.shape
    kv_width = all_width // 2
    head = lax.axis_index("head").astype(jnp.int32)[None]
    order = token_order[None]
    shape = jax.ShapeDtypeStruct

    is_first = head[0] == 0
    lower = jnp.concatenate([key_states[:, :kv_width], value_states[:, :kv_width]], axis=1)
    upper = jnp.concatenate([key_states[:, kv_width:], value_states[:, kv_width:]], axis=1)
    got = swap_head(jnp.where(is_first, upper, lower))
    row_pack = pl.pallas_call(
        pack_rows_kernel,
        out_shape=shape((2 * rows + AUX, width), jnp.bfloat16),
        in_specs=[VMEM_SPEC] * 6,
        out_specs=VMEM_SPEC,
    )(queries, attn_out, grad_out, log_sum_exp, order, position[None])
    keep = jnp.where(is_first, lower, upper)
    places = jnp.concatenate([*split_place(token_order), jnp.zeros((2 * kv_width - 2 * rows,), jnp.bfloat16)])
    col_pack = jnp.concatenate(
        [
            jnp.where(is_first, keep, got),
            jnp.where(is_first, got, keep),
            jnp.broadcast_to(places[None], (AUX, 2 * kv_width)),
        ],
        axis=0,
    )

    row_ahead = shifted(row_pack, 1, 0)
    row_behind = shifted(row_pack, -1, 0)
    row_two_q = shifted(row_ahead[:rows], 1, 0)
    row_two_g = shifted(row_behind[rows:], -1, 0)
    ahead = shifted(col_pack, 0, 1)
    behind = shifted(col_pack, 0, -1)
    across = shifted(col_pack, 0, 4)
    ahead_pair = shifted(jnp.concatenate([col_pack, ahead], axis=0), 0, 2)
    behind_pair = shifted(jnp.concatenate([col_pack, behind], axis=0), 0, -2)

    size = 2 * half + AUX
    first_rows = [row_pack, row_ahead, row_behind]
    first_places = tuple(((r, 0), (r, rows), (r, 2 * rows)) for r in range(3))
    two_rows = [row_two_q, row_two_g]
    near = [col_pack, ahead, behind]
    near_places = ((0, 0), (1, 0), (2, 0))
    near_shifts = (0, 1, -1)
    far = [ahead_pair, behind_pair]
    far_places = ((0, 0), (0, size), (1, 0), (1, size))
    far_shifts = (2, 3, -2, -3)
    if FOUR_NEAR:
        near.append(across)
        near_places += ((3, 0),)
        near_shifts += (4,)
    else:
        far.append(across)
        far_places += ((2, 0),)
        far_shifts += (4,)
    two_place = ((0, 0), (1, 0), (1, rows))
    last_place = ((3, 0), (4, 0), (4, rows))

    dq_first, kv_near = call_grads(first_rows, first_places, near, near_places, (), (), False, False)
    dq_two, near_parts = call_grads(two_rows, (two_place,), near, near_places, (), kv_near, False, True)
    dq_parts, far_parts = call_grads(
        first_rows + two_rows, first_places + (last_place,), far, far_places, (*dq_first, *dq_two), (), True, True
    )

    parts = dict(zip(near_shifts + far_shifts, (*near_parts, *far_parts)))
    dkv = parts.pop(0).astype(jnp.float32)
    for s, part in parts.items():
        back = shifted(part, 0, -s)
        dkv = dkv + back.astype(jnp.float32)
    dq = dq_parts[0].astype(jnp.float32)
    for s, part in list(zip(ROW_SHIFTS, dq_parts))[1:]:
        back = shifted(part, -s, 0)
        dq = dq + back.astype(jnp.float32)
    grad_queries = dq.astype(jnp.bfloat16)

    dkv = dkv.astype(jnp.bfloat16)
    send_back = jnp.where(is_first, dkv[half:], dkv[:half])
    mine = jnp.where(is_first, dkv[:half], dkv[half:])
    other = swap_head(send_back)
    low = jnp.where(is_first, mine, other)
    high = jnp.where(is_first, other, mine)
    grad_keys = jnp.concatenate([low[:, :kv_width], high[:, :kv_width]], axis=1)
    grad_values = jnp.concatenate([low[:, kv_width:], high[:, kv_width:]], axis=1)
    return grad_queries, grad_keys, grad_values


FOUR_NEAR = True


def solution(mesh):
    in_specs = (
        P("ctx", "head"),
        P(("ctx", "head"), None),
        P(("ctx", "head"), None),
        P("ctx", "head"),
        P("ctx", "head"),
        P("head", "ctx"),
        P("ctx"),
        P("ctx"),
    )
    out_specs = (P("ctx", "head"), P(("ctx", "head"), None), P(("ctx", "head"), None))
    return jax.shard_map(shards, mesh=mesh, in_specs=in_specs, out_specs=out_specs, check_vma=False)
```

```python
import functools
import math

import jax
import jax.numpy as jnp
from jax import lax
from jax.experimental import pallas as pl
from jax.experimental.pallas import tpu as pltpu
from jax.sharding import PartitionSpec as P


HEAD_DIM = 128
QUARTERS = 4
GRID_Y = 4
GRID_Z = 8
ROW_SHIFTS = (0, 1, -1, 2)
AUX = 8
SPLIT = 1
LOG2E = math.log2(math.e)
SCALE = HEAD_DIM ** (-0.5)

VMEM_SPEC = pl.BlockSpec(memory_space=pltpu.VMEM)
SMEM_SPEC = pl.BlockSpec(memory_space=pltpu.SMEM)
NT = (((1,), (1,)), ((), ()))
NN = (((1,), (0,)), ((), ()))


def dot(a, b, dims):
    return lax.dot_general(a, b, dims, preferred_element_type=jnp.float32)


def shifted(value, along_y, along_z):
    pairs = []
    for y in range(GRID_Y):
        for z in range(GRID_Z):
            source = ((y + along_y) % GRID_Y) * GRID_Z + (z + along_z) % GRID_Z
            for quarter in range(QUARTERS):
                pairs.append((source * QUARTERS + quarter, (y * GRID_Z + z) * QUARTERS + quarter))
    return lax.ppermute(value, "ctx", pairs)


def swap_head(value):
    return lax.ppermute(value, "head", [(0, 1), (1, 0)])


def split_three(x):
    high = x.astype(jnp.bfloat16)
    rest = x - high.astype(jnp.float32)
    middle = rest.astype(jnp.bfloat16)
    low = (rest - middle.astype(jnp.float32)).astype(jnp.bfloat16)
    return high, middle, low


def split_place(x):
    return (x >> 7).astype(jnp.float32).astype(jnp.bfloat16), (x & 127).astype(jnp.float32).astype(jnp.bfloat16)


def pack_rows_kernel(q_ref, o_ref, g_ref, lse_ref, order_ref, position_ref, out_ref):
    rows, width = q_ref.shape
    out_ref[0:rows, :] = q_ref[...]
    out_ref[rows : 2 * rows, :] = g_ref[...]
    base = 2 * rows
    out_ref[base : base + AUX, :] = jnp.zeros((AUX, width), jnp.bfloat16)
    order = order_ref[...]
    first = order - position_ref[...]
    places = split_place(first) + split_place(order)
    for at, part in enumerate(places):
        out_ref[base + 6 : base + 7, at * rows : (at + 1) * rows] = part
    product = q_ref.shape[1] // HEAD_DIM
    for h in range(product):
        span = slice(h * HEAD_DIM, (h + 1) * HEAD_DIM)
        both = g_ref[:, span].astype(jnp.float32) * o_ref[:, span].astype(jnp.float32)
        out_dot = jnp.sum(jnp.transpose(both), axis=0, keepdims=True)
        for at, part in enumerate(split_three(lse_ref[h : h + 1, :])):
            out_ref[base + at : base + at + 1, span] = part
        for at, part in enumerate(split_three(out_dot)):
            out_ref[base + 3 + at : base + 4 + at, span] = part


def grads_kernel(row_places, col_places, dq_given, kv_given, dq_final, kv_final, *refs):
    n_rows = len(row_places)
    n_cols = len(col_places)
    refs = list(refs)

    def take(count):
        taken, refs[:] = refs[:count], refs[count:]
        return taken

    row_refs = take(1 + max(at for place in row_places for at, _ in place))
    col_refs = take(1 + max(at for at, _ in col_places))
    dq_in = take(dq_given)
    kv_in = take(2 * kv_given)
    dq_refs = take(n_rows if dq_final else 1)
    dkv_refs = take(n_cols if kv_final else 2)
    qs, gs, lse_s, dot_s, first_s, last_s, ks, vs, kts = take(9)
    dqt = take(1)[0] if dq_final else dq_refs[0]
    dk, dv = take(2) if kv_final else dkv_refs
    starts, listed, counts, limits = take(4)
    rows = 128
    heads = row_refs[0].shape[1] // HEAD_DIM
    kv_heads = col_refs[0].shape[1] // HEAD_DIM // 2
    group = heads // kv_heads
    wide = group * rows

    eye_i = lax.broadcasted_iota(jnp.int32, (rows, rows), 0)
    eye_j = lax.broadcasted_iota(jnp.int32, (rows, rows), 1)
    eye = (eye_i == eye_j).astype(jnp.float32).astype(jnp.bfloat16)

    col_starts = []
    for c, (at, base) in enumerate(col_places):
        ref = col_refs[at]
        for j in range(kv_heads):
            k = ref[base : base + rows, j * HEAD_DIM : (j + 1) * HEAD_DIM]
            ks[c, j] = k
            vs[c, j] = ref[base : base + rows, (kv_heads + j) * HEAD_DIM : (kv_heads + j + 1) * HEAD_DIM]
            kts[c, j] = dot(eye, k, NT).astype(jnp.bfloat16)
        aux = ref[base + rows : base + rows + AUX, :].astype(jnp.float32)
        place = (aux[0:1, 0:rows] * 128.0 + aux[0:1, rows : 2 * rows]).astype(jnp.int32)
        col_starts.append(jnp.min(place))
        starts[c] = col_starts[-1]
    for r, ((q_at, q_base), (g_at, g_base), (at, base)) in enumerate(row_places):
        for h in range(heads):
            span = slice(h * HEAD_DIM, (h + 1) * HEAD_DIM)
            qs[r, span, :] = row_refs[q_at][q_base : q_base + rows, span]
            gs[r, span, :] = row_refs[g_at][g_base : g_base + rows, span]
        aux = row_refs[at][base : base + AUX, :].astype(jnp.float32)
        lse = (aux[0:1] + aux[1:2]) + aux[2:3]
        out_dot = (aux[3:4] + aux[4:5]) + aux[5:6]
        lse_s[r] = lse * LOG2E
        dot_s[r] = out_dot
        first = aux[6:7, 0:rows] * 128.0 + aux[6:7, rows : 2 * rows]
        last = aux[6:7, 2 * rows : 3 * rows] * 128.0 + aux[6:7, 3 * rows : 4 * rows]
        first = first.astype(jnp.int32)
        last = last.astype(jnp.int32)
        for g in range(group):
            first_s[r, :, g * rows : (g + 1) * rows] = first
            last_s[r, :, g * rows : (g + 1) * rows] = last
        most = jnp.max(last)
        least = jnp.min(first)
        count = jnp.int32(0)
        for c in range(n_cols):
            listed[r, count] = c
            some = (col_starts[c] <= most) & (col_starts[c] + (rows - 1) >= least)
            count = count + some.astype(jnp.int32)
        counts[r] = count
        limits[0, r] = jnp.min(last)
        limits[1, r] = jnp.max(first)
    filled = 0
    for old in dq_in:
        dqt[filled : filled + old.shape[0]] = old[...]
        filled += old.shape[0]
    if filled == 0:
        dqt[...] = jnp.zeros_like(dqt)
    if kv_given:
        dk[...] = kv_in[0][...]
        dv[...] = kv_in[1][...]
    else:
        dk[...] = jnp.zeros_like(dk)
        dv[...] = jnp.zeros_like(dv)

    def pair(r, one, two, start_one, start_two, masked):
        part_wide = wide // SPLIT
        heads_starts = (start_one, start_two)
        if masked:
            along = lax.broadcasted_iota(jnp.int32, (rows, part_wide), 0)
            last = last_s[r, :, 0:part_wide]
            first = first_s[r, :, 0:part_wide]
            visible = [(along + start <= last) & (along + start >= first) for start in heads_starts]
        for j in range(kv_heads):
            keys = jnp.concatenate([ks[one, j], ks[two, j]], axis=0)
            values = jnp.concatenate([vs[one, j], vs[two, j]], axis=0)
            keys_turned = jnp.concatenate([kts[one, j], kts[two, j]], axis=1)
            value_update = None
            for piece in range(SPLIT):
                low = j * wide + piece * part_wide
                span = slice(low, low + part_wide)
                q = qs[r, span, :]
                g = gs[r, span, :]
                scores = dot(keys, q, NT)
                prob_grad = dot(values, g, NT)
                lse = lse_s[r, :, span]
                out_dot = dot_s[r, :, span]
                probs_both = []
                grads_both = []
                for at in range(2):
                    part = slice(at * rows, (at + 1) * rows)
                    probs = jnp.exp2(scores[part] * (SCALE * LOG2E) - lse)
                    if masked:
                        probs = jnp.where(visible[at], probs, 0.0)
                    grads_both.append((probs * (prob_grad[part] - out_dot) * SCALE).astype(jnp.bfloat16))
                    probs_both.append(probs.astype(jnp.bfloat16))
                probs = jnp.concatenate(probs_both, axis=0)
                score_grad = jnp.concatenate(grads_both, axis=0)
                piece_value = dot(probs, g, NN)
                piece_key = dot(score_grad, q, NN)
                value_update = piece_value if value_update is None else value_update + piece_value
                key_update = piece_key if piece == 0 else key_update + piece_key
                here = slice(piece * part_wide, (piece + 1) * part_wide)
                dqt[r, j, :, here] += dot(keys_turned, score_grad, NN)
            dv[one, j] += value_update[:rows]
            dv[two, j] += value_update[rows:]
            dk[one, j] += key_update[:rows]
            dk[two, j] += key_update[rows:]

    def row_block(r, carry):
        count = counts[r]

        def trip(at, inner):
            one = listed[r, 2 * at]
            both = 2 * at + 1 < count
            two = jnp.where(both, listed[r, 2 * at + 1], one)
            start_one = starts[one]
            start_two = jnp.where(both, starts[two], 1 << 20)
            top = jnp.maximum(start_one, start_two) + (rows - 1)
            whole = (top <= limits[0, r]) & (jnp.minimum(start_one, start_two) >= limits[1, r])
            pl.when(whole)(lambda: pair(r, one, two, start_one, start_two, False))
            pl.when(jnp.logical_not(whole))(lambda: pair(r, one, two, start_one, start_two, True))
            return inner

        return lax.fori_loop(0, (count + 1) // 2, trip, carry)

    lax.fori_loop(0, n_rows, row_block, 0)

    for c, ref in enumerate(dkv_refs if kv_final else ()):
        for j in range(kv_heads):
            ref[:, j * HEAD_DIM : (j + 1) * HEAD_DIM] = dk[c, j].astype(jnp.bfloat16)
            ref[:, (kv_heads + j) * HEAD_DIM : (kv_heads + j + 1) * HEAD_DIM] = dv[c, j].astype(jnp.bfloat16)
    for r, ref in enumerate(dq_refs if dq_final else ()):
        for j in range(kv_heads):
            for g in range(group):
                part = dqt[r, j, :, g * rows : (g + 1) * rows].astype(jnp.bfloat16)
                h = j * group + g
                ref[:, h * HEAD_DIM : (h + 1) * HEAD_DIM] = dot(eye, part, NT).astype(jnp.bfloat16)


def call_grads(row_packs, row_places, col_packs, col_places, dq_in, kv_in, dq_final, kv_final):
    rows = 128
    n_rows, n_cols = len(row_places), len(col_places)
    width, all_kv = row_packs[0].shape[1], col_packs[0].shape[1]
    kv_heads = all_kv // HEAD_DIM // 2
    heads = width // HEAD_DIM
    wide = heads // kv_heads * rows
    shape = jax.ShapeDtypeStruct
    dq_shape = (n_rows, kv_heads, HEAD_DIM, wide)
    kv_shape = (n_cols, kv_heads, rows, HEAD_DIM)
    out_shape = (shape(dq_shape, jnp.float32),)
    if dq_final:
        out_shape = (shape((rows, width), jnp.bfloat16),) * n_rows
    if kv_final:
        out_shape += (shape((rows, all_kv), jnp.bfloat16),) * n_cols
    else:
        out_shape += (shape(kv_shape, jnp.float32),) * 2
    operands = (*row_packs, *col_packs, *dq_in, *kv_in)
    scratch = [
        pltpu.VMEM((n_rows, heads * rows, HEAD_DIM), jnp.bfloat16),
        pltpu.VMEM((n_rows, heads * rows, HEAD_DIM), jnp.bfloat16),
        pltpu.VMEM((n_rows, 1, heads * rows), jnp.float32),
        pltpu.VMEM((n_rows, 1, heads * rows), jnp.float32),
        pltpu.VMEM((n_rows, 1, wide), jnp.int32),
        pltpu.VMEM((n_rows, 1, wide), jnp.int32),
        pltpu.VMEM((n_cols, kv_heads, rows, HEAD_DIM), jnp.bfloat16),
        pltpu.VMEM((n_cols, kv_heads, rows, HEAD_DIM), jnp.bfloat16),
        pltpu.VMEM((n_cols, kv_heads, HEAD_DIM, rows), jnp.bfloat16),
    ]
    if dq_final:
        scratch += [pltpu.VMEM(dq_shape, jnp.float32)]
    if kv_final:
        scratch += [pltpu.VMEM(kv_shape, jnp.float32)] * 2
    scratch += [
        pltpu.SMEM((n_cols,), jnp.int32),
        pltpu.SMEM((n_rows, n_cols + 1), jnp.int32),
        pltpu.SMEM((n_rows,), jnp.int32),
        pltpu.SMEM((2, n_rows), jnp.int32),
    ]
    body = functools.partial(
        grads_kernel, row_places, col_places, len(dq_in), bool(kv_in), dq_final, kv_final
    )
    outs = pl.pallas_call(
        body,
        out_shape=out_shape,
        in_specs=[VMEM_SPEC] * len(operands),
        out_specs=(VMEM_SPEC,) * len(out_shape),
        scratch_shapes=scratch,
        compiler_params=pltpu.CompilerParams(vmem_limit_bytes=40 * 1024 * 1024),
    )(*operands)
    cut = n_rows if dq_final else 1
    return outs[:cut], outs[cut:]


def shards(queries, key_states, value_states, attn_out, grad_out, log_sum_exp, token_order, position):
    rows, width = queries.shape
    half, all_width = key_states.shape
    kv_width = all_width // 2
    head = lax.axis_index("head").astype(jnp.int32)[None]
    order = token_order[None]
    shape = jax.ShapeDtypeStruct

    is_first = head[0] == 0
    lower = jnp.concatenate([key_states[:, :kv_width], value_states[:, :kv_width]], axis=1)
    upper = jnp.concatenate([key_states[:, kv_width:], value_states[:, kv_width:]], axis=1)
    got = swap_head(jnp.where(is_first, upper, lower))
    row_pack = pl.pallas_call(
        pack_rows_kernel,
        out_shape=shape((2 * rows + AUX, width), jnp.bfloat16),
        in_specs=[VMEM_SPEC] * 6,
        out_specs=VMEM_SPEC,
    )(queries, attn_out, grad_out, log_sum_exp, order, position[None])
    keep = jnp.where(is_first, lower, upper)
    places = jnp.concatenate([*split_place(token_order), jnp.zeros((2 * kv_width - 2 * rows,), jnp.bfloat16)])
    col_pack = jnp.concatenate(
        [
            jnp.where(is_first, keep, got),
            jnp.where(is_first, got, keep),
            jnp.broadcast_to(places[None], (AUX, 2 * kv_width)),
        ],
        axis=0,
    )

    row_ahead = shifted(row_pack, 1, 0)
    row_behind = shifted(row_pack, -1, 0)
    row_two_q = shifted(row_ahead[:rows], 1, 0)
    row_two_g = shifted(row_behind[rows:], -1, 0)
    ahead = shifted(col_pack, 0, 1)
    behind = shifted(col_pack, 0, -1)
    across = shifted(col_pack, 0, 4)
    ahead_pair = shifted(jnp.concatenate([col_pack, ahead], axis=0), 0, 2)
    behind_pair = shifted(jnp.concatenate([col_pack, behind], axis=0), 0, -2)

    size = 2 * half + AUX
    first_rows = [row_pack, row_ahead, row_behind]
    first_places = tuple(((r, 0), (r, rows), (r, 2 * rows)) for r in range(3))
    two_rows = [row_two_q, row_two_g]
    near = [col_pack, ahead, behind]
    near_places = ((0, 0), (1, 0), (2, 0))
    near_shifts = (0, 1, -1)
    far = [ahead_pair, behind_pair]
    far_places = ((0, 0), (0, size), (1, 0), (1, size))
    far_shifts = (2, 3, -2, -3)
    if FOUR_NEAR:
        near.append(across)
        near_places += ((3, 0),)
        near_shifts += (4,)
    else:
        far.append(across)
        far_places += ((2, 0),)
        far_shifts += (4,)
    two_place = ((0, 0), (1, 0), (1, rows))
    last_place = ((3, 0), (4, 0), (4, rows))

    dq_first, kv_near = call_grads(
        first_rows, first_places, near, near_places, (), (), False, False
    )
    dq_two, near_parts = call_grads(
        two_rows, (two_place,), near, near_places, (), kv_near, False, True
    )
    dq_parts, far_parts = call_grads(
        first_rows + two_rows,
        first_places + (last_place,),
        far,
        far_places,
        (*dq_first, *dq_two),
        (),
        True,
        True,
    )

    parts = dict(zip(near_shifts + far_shifts, (*near_parts, *far_parts)))
    dkv = parts.pop(0).astype(jnp.float32)
    for s, part in parts.items():
        back = shifted(part, 0, -s)
        dkv = dkv + back.astype(jnp.float32)
    dq = dq_parts[0].astype(jnp.float32)
    for s, part in list(zip(ROW_SHIFTS, dq_parts))[1:]:
        back = shifted(part, -s, 0)
        dq = dq + back.astype(jnp.float32)
    grad_queries = dq.astype(jnp.bfloat16)

    dkv = dkv.astype(jnp.bfloat16)
    send_back = jnp.where(is_first, dkv[half:], dkv[:half])
    mine = jnp.where(is_first, dkv[:half], dkv[half:])
    other = swap_head(send_back)
    low = jnp.where(is_first, mine, other)
    high = jnp.where(is_first, other, mine)
    grad_keys = jnp.concatenate([low[:, :kv_width], high[:, :kv_width]], axis=1)
    grad_values = jnp.concatenate([low[:, kv_width:], high[:, kv_width:]], axis=1)
    return grad_queries, grad_keys, grad_values


FOUR_NEAR = True


def solution(mesh):
    in_specs = (
        P("ctx", "head"),
        P(("ctx", "head"), None),
        P(("ctx", "head"), None),
        P("ctx", "head"),
        P("ctx", "head"),
        P("head", "ctx"),
        P("ctx"),
        P("ctx"),
    )
    out_specs = (P("ctx", "head"), P(("ctx", "head"), None), P(("ctx", "head"), None))
    return jax.shard_map(shards, mesh=mesh, in_specs=in_specs, out_specs=out_specs, check_vma=False)
```
